32 devices in a mesh: groups: 2 (over y), seq: 4 (over z), tensor: 4 (over x, core).
Axes of the slice: x: 2, y: 2, z: 4, core: 2. Of those that a mesh axis runs over, the one named last changes fastest.
Arguments:
- video_query: bfloat16 [1024, 4096], P(('groups', 'seq'), 'tensor'), parts along dimension 0, may hold values from -21 to 21
- video_key: bfloat16 [1024, 4096], P(('groups', 'seq'), 'tensor'), parts along dimension 0, may hold values from -21 to 21
- video_value: bfloat16 [1024, 4096], P(('groups', 'seq'), 'tensor'), parts along dimension 0, may hold values from -6 to 6
- video_stream: bfloat16 [1024, 4096], P(('groups', 'seq'), 'tensor'), parts along dimension 0, may hold values from -6 to 6
- out_weight: bfloat16 [4096, 4096], P('tensor'), may hold values from -0.09375 to 0.09375
- cross_query: bfloat16 [1024, 2048], P(('groups', 'seq'), 'tensor'), parts along dimension 0, may hold values from -21 to 21
- audio_key: bfloat16 [128, 2048], P(('groups', 'seq'), 'tensor'), parts along dimension 0, may hold values from -21 to 21
- audio_value: bfloat16 [128, 2048], P(('groups', 'seq'), 'tensor'), parts along dimension 0, may hold values from -6 to 6
- audio_query: bfloat16 [128, 2048], P(('groups', 'seq'), 'tensor'), parts along dimension 0, may hold values from -21 to 21
- cross_key: bfloat16 [1024, 2048], P(('groups', 'seq'), 'tensor'), parts along dimension 0, may hold values from -21 to 21
- cross_value: bfloat16 [1024, 2048], P(('groups', 'seq'), 'tensor'), parts along dimension 0, may hold values from -6 to 6
Outputs:
- video_next: bfloat16 [1024, 4096], P(('groups', 'seq'), 'tensor'), parts along dimension 0
- video_cross: bfloat16 [1024, 2048], P(('groups', 'seq'), 'tensor'), parts along dimension 0
- audio_cross: bfloat16 [128, 2048], P(('groups', 'seq'), 'tensor'), parts along dimension 0
The draws below stay inside these ranges and needn't reach their ends.
There are 2 independent parts, one for each index of `groups`. The reference program is written for one: setup_inputs(seed, part) draws one part's arguments, and reference() takes and returns one part's arrays. A program takes and returns all parts, laid end to end along the dimension named above; an argument that names none is the same for every part. Nothing has to cross between parts.
All inputs are finite; a program needn't handle non-finite values.
Results may differ from the reference program's by a relative error of at most 0.012.
Values may be sent and summed in bfloat16 or wider, within the bound.
A program may use at most 64 MiB of HBM per device.

```python
import math
import jax
import jax.numpy as jnp
from jax import lax

DV = 4096
DA = 2048
HV = 32
HA = 16
HD = 128
VT = 512
AT = 64


def paired(key, query_rows, key_rows, width, salt):
    subkeys = jax.random.split(jax.random.fold_in(key, salt), 2)
    queries = jnp.clip(1.5 * jax.random.normal(subkeys[0], (query_rows, width), jnp.float32), -6.0, 6.0)
    keyset = jnp.clip(1.5 * jax.random.normal(subkeys[1], (key_rows, width), jnp.float32), -6.0, 6.0)
    return (queries, keyset)


def draw_video_query(key, part):
    return paired(key, VT, VT, DV, 11)[0].astype(jnp.bfloat16)


def draw_video_key(key, part):
    return paired(key, VT, VT, DV, 11)[1].astype(jnp.bfloat16)


def draw_cross_query(key, part):
    return paired(key, VT, AT, DA, 23)[0].astype(jnp.bfloat16)


def draw_audio_key(key, part):
    return paired(key, VT, AT, DA, 23)[1].astype(jnp.bfloat16)


def draw_audio_query(key, part):
    return paired(key, AT, VT, DA, 37)[0].astype(jnp.bfloat16)


def draw_cross_key(key, part):
    return paired(key, AT, VT, DA, 37)[1].astype(jnp.bfloat16)


def block_levels(stream_key, shape, pieces, low, largest):
    def one(position, shards_of):
        heights = jax.random.uniform(jax.random.fold_in(jax.random.fold_in(stream_key, 6), position), (shards_of,), jnp.float32, low / len(pieces), largest / len(pieces))
        return jnp.repeat(jnp.exp(heights), shape[position] // shards_of).reshape((-1,) + (1,) * (len(shape) - position - 1))

    factor_of = one(*pieces[0])
    for cut in pieces[1:]:
        factor_of = factor_of * one(*cut)
    return factor_of


def bell_draw(key, dims, spread, limit, pieces=(), held_as=jnp.bfloat16):
    entries = spread * jax.random.normal(key, dims, jnp.float32)
    if pieces:
        entries = entries * block_levels(key, dims, pieces, -0.22, 0.18)
    return jnp.clip(entries, -limit, limit).astype(held_as)


def setup_inputs(seed: int = 0, part: int = 0) -> dict:
    arg_keys = jax.random.split(jax.random.key(seed), 12)
    part_keys = jax.random.split(jax.random.fold_in(arg_keys[11], part), 12)
    return {
        "video_query": draw_video_query(jax.random.fold_in(jax.random.fold_in(arg_keys[11], part), 71), part),
        "video_key": draw_video_key(jax.random.fold_in(jax.random.fold_in(arg_keys[11], part), 71), part),
        "video_value": bell_draw(part_keys[2], (VT, DV), 1.0, 6.0, ((0, 4), (1, 4))),
        "video_stream": bell_draw(part_keys[3], (VT, DV), 1.0, 6.0, ((0, 4), (1, 4))),
        "out_weight": bell_draw(arg_keys[4], (DV, DV), DV ** -0.5, 0.09375, ((0, 4),)),
        "cross_query": draw_cross_query(jax.random.fold_in(jax.random.fold_in(arg_keys[11], part), 71), part),
        "audio_key": draw_audio_key(jax.random.fold_in(jax.random.fold_in(arg_keys[11], part), 71), part),
        "audio_value": bell_draw(part_keys[7], (AT, DA), 1.0, 6.0, ((0, 4), (1, 4))),
        "audio_query": draw_audio_query(jax.random.fold_in(jax.random.fold_in(arg_keys[11], part), 71), part),
        "cross_key": draw_cross_key(jax.random.fold_in(jax.random.fold_in(arg_keys[11], part), 71), part),
        "cross_value": bell_draw(part_keys[10], (VT, DA), 1.0, 6.0, ((0, 4), (1, 4))),
    }


def attend(queries, keyset, values, head_count):
    query_rows = queries.shape[0]
    key_rows = keyset.shape[0]
    query_head = queries.reshape(query_rows, head_count, HD).transpose(1, 0, 2)
    key_head = keyset.reshape(key_rows, head_count, HD).transpose(1, 0, 2)
    value_head = values.reshape(key_rows, head_count, HD).transpose(1, 0, 2)

    def single(operands):
        query_one, key_one, value_one = operands
        scores = jnp.dot(query_one, key_one.T, preferred_element_type=jnp.float32) * (1.0 / math.sqrt(HD))
        row_max = lax.optimization_barrier(jnp.max(scores, axis=1, keepdims=True))
        raised = jnp.exp(scores - row_max)
        row_sum = lax.optimization_barrier(jnp.sum(raised, axis=1, keepdims=True))
        weights = raised.astype(jnp.bfloat16)
        return jnp.dot(weights, value_one, preferred_element_type=jnp.float32) / row_sum
    result = lax.map(single, (query_head, key_head, value_head))
    return result.transpose(1, 0, 2).reshape(query_rows, head_count * HD)

def reference(video_query, video_key, video_value, video_stream, out_weight, cross_query, audio_key, audio_value, audio_query, cross_key, cross_value):
    video_heads = attend(video_query, video_key, video_value, HV).astype(jnp.bfloat16)
    projected = jnp.dot(video_heads, out_weight, preferred_element_type=jnp.float32)
    video_next = (video_stream.astype(jnp.float32) + projected).astype(jnp.bfloat16)
    video_cross = attend(cross_query, audio_key, audio_value, HA).astype(jnp.bfloat16)
    audio_cross = attend(audio_query, cross_key, cross_value, HA).astype(jnp.bfloat16)
    return (video_next, video_cross, audio_cross)
```

```python
import functools
import math

import jax
import jax.numpy as jnp
from jax import lax
from jax.experimental import pallas as pl
from jax.experimental.pallas import tpu as pltpu
from jax.sharding import PartitionSpec as P

HD = 128


def blank_state(query_rows, head_count):
    return (
        jnp.full((head_count, query_rows), -1e30, jnp.float32),
        jnp.zeros((head_count, query_rows), jnp.float32),
        jnp.zeros((head_count, query_rows, HD), jnp.float32),
    )


def absorb(carried, queries, keyset, values, head_count):
    running, row_sum, numerator = carried
    query_rows = queries.shape[0]
    key_rows = keyset.shape[0]
    factor = 1.0 / math.sqrt(HD)
    query_heads = queries.reshape(query_rows, head_count, HD)
    for offset in range(0, key_rows, 1024):
        width_keys = min(1024, key_rows - offset)
        key_block = keyset[offset : offset + width_keys].reshape(width_keys, head_count, HD)
        value_block = values[offset : offset + width_keys].reshape(width_keys, head_count, HD)
        scores = (
            jnp.einsum("qhd,khd->hqk", query_heads, key_block, preferred_element_type=jnp.float32)
            * factor
        )
        highest = jnp.maximum(running, jnp.max(scores, axis=2))
        raised = jnp.exp(scores - highest[:, :, None])
        shrink = jnp.exp(running - highest)
        row_sum = row_sum * shrink + jnp.sum(raised, axis=2)
        numerator = numerator * shrink[:, :, None] + jnp.einsum(
            "hqk,khd->hqd",
            raised.astype(jnp.bfloat16),
            value_block,
            preferred_element_type=jnp.float32,
        )
        running = highest
    return (running, row_sum, numerator)


def finish(carried, head_count):
    running, row_sum, numerator = carried
    result = numerator / row_sum[:, :, None]
    return result.transpose(1, 0, 2).reshape(result.shape[1], head_count * HD).astype(jnp.bfloat16)


def local(
    video_query,
    video_key,
    video_value,
    video_stream,
    out_weight,
    cross_query,
    audio_key,
    audio_value,
    audio_query,
    cross_key,
    cross_value,
):
    local_heads = video_query.shape[1] // HD
    query_rows = video_query.shape[0]
    pieces = (
        lax.all_gather(video_key, "seq", axis=0, tiled=True),
        lax.all_gather(video_value, "seq", axis=0, tiled=True),
    )
    carried_video = absorb(
        blank_state(query_rows, local_heads), video_query, pieces[0], pieces[1], local_heads
    )
    attended = finish(carried_video, local_heads)
    projected = jnp.dot(attended, out_weight, preferred_element_type=jnp.float32)
    summed = lax.psum_scatter(
        projected.astype(jnp.bfloat16), "tensor", scatter_dimension=1, tiled=True
    ).astype(jnp.float32)
    video_next = (video_stream.astype(jnp.float32) + summed).astype(jnp.bfloat16)
    cross_heads = cross_query.shape[1] // HD
    every_key, every_value = (
        lax.all_gather(audio_key, "seq", axis=0, tiled=True),
        lax.all_gather(audio_value, "seq", axis=0, tiled=True),
    )
    carried_audio = absorb(
        blank_state(cross_query.shape[0], cross_heads),
        cross_query,
        every_key,
        every_value,
        cross_heads,
    )
    video_cross = finish(carried_audio, cross_heads)
    pieces = (
        lax.all_gather(cross_key, "seq", axis=0, tiled=True),
        lax.all_gather(cross_value, "seq", axis=0, tiled=True),
    )
    carried_cross = absorb(
        blank_state(audio_query.shape[0], cross_heads),
        audio_query,
        pieces[0],
        pieces[1],
        cross_heads,
    )
    audio_cross = finish(carried_cross, cross_heads)
    return (video_next, video_cross, audio_cross)


MESH = pl.DeviceIdType.MESH
NT = (((1,), (1,)), ((), ()))
WIDE = 256


def softmax_parts(queries, keyset, values):
    scores = lax.dot_general(queries, keyset, NT, preferred_element_type=jnp.float32) * (
        1.0 / math.sqrt(HD)
    )
    highest = jnp.max(scores, axis=1, keepdims=True)
    raised = jnp.exp(scores - highest)
    row_sum = jnp.sum(raised, axis=1, keepdims=True)
    numerator = jnp.dot(raised.astype(jnp.bfloat16), values, preferred_element_type=jnp.float32)
    return highest, row_sum, numerator


def block_kernel(
    seq,
    tensor,
    vq,
    vk,
    vv,
    vs,
    weight,
    cq,
    ak,
    av,
    aq,
    ck,
    cv,
    next_ref,
    vcross_ref,
    across_ref,
    qkv,
    heads_out,
    gathered,
    audio,
    partial,
    stats,
    partial_in,
    stats_in,
    cq_v,
    ck_v,
    cv_v,
    stream_v,
    weight_v,
    total,
    pair_out,
    pair_in,
    far_out,
    far_in,
    qkv_send,
    qkv_recv,
    own_sem,
    out_send,
    out_recv,
    audio_send,
    audio_recv,
    audio_own,
    part_send,
    part_recv,
    stat_send,
    stat_recv,
    load_sem,
    weight_sem,
    pair_send,
    pair_recv,
    far_send,
    far_recv,
):
    rows = vq.shape[0]
    share = vq.shape[1] // HD // seq
    cross_heads = cq.shape[1] // HD
    audio_rows = aq.shape[0]
    chips = tensor // 2
    width = next_ref.shape[1]
    pieces = width // WIDE
    me = lax.axis_index("seq")
    place = lax.axis_index("tensor")
    core = lax.rem(place, 2)
    chip = place // 2
    sibling = chip * 2 + (1 - core)
    peers = [lax.rem(me + d, seq) for d in range(1, seq)]
    far_chips = [lax.rem(chip + d, chips) for d in range(chips)]

    my_rows = pl.ds(pl.multiple_of(me * rows, rows), rows)
    my_audio = pl.ds(pl.multiple_of(me * audio_rows, audio_rows), audio_rows)

    def head_cols(owner, h):
        return pl.ds(pl.multiple_of((owner * share + h) * HD, HD), HD)

    local_copies = []
    for h in range(share):
        for kind, ref in enumerate((vk, vv, vq)):
            copy = pltpu.make_async_copy(
                ref.at[:, head_cols(me, h)], qkv.at[kind, h, my_rows], own_sem.at[kind, h]
            )
            copy.start()
            local_copies.append(copy)
    audio_copies = []
    for kind, ref in enumerate((ak, av, aq)):
        copy = pltpu.make_async_copy(ref, audio.at[kind, my_audio], audio_own.at[kind])
        copy.start()
        audio_copies.append(copy)
    loads = []
    for i, (ref, dst) in enumerate(((cq, cq_v), (ck, ck_v), (cv, cv_v), (vs, stream_v))):
        copy = pltpu.make_async_copy(ref, dst, load_sem.at[i])
        copy.start()
        loads.append(copy)

    barrier = pltpu.get_barrier_semaphore()
    for p in peers:
        pl.semaphore_signal(barrier, inc=1, device_id={"seq": p}, device_id_type=MESH)
    pl.semaphore_signal(barrier, inc=1, device_id={"tensor": sibling}, device_id_type=MESH)
    for d in range(1, chips):
        pl.semaphore_signal(
            barrier, inc=1, device_id={"tensor": far_chips[d] * 2 + core}, device_id_type=MESH
        )
    pl.semaphore_wait(barrier, seq - 1 + chips)

    sends = []

    def send_heads(h):
        for kind, ref in enumerate((vk, vv, vq)):
            for p in peers:
                copy = pltpu.make_async_remote_copy(
                    src_ref=ref.at[:, head_cols(p, h)],
                    dst_ref=qkv.at[kind, h, my_rows],
                    send_sem=qkv_send.at[kind, h, p],
                    recv_sem=qkv_recv.at[kind, h, me],
                    device_id={"seq": p},
                    device_id_type=MESH,
                )
                copy.start()
                sends.append(copy)

    send_heads(0)
    for kind, ref in enumerate((ak, av, aq)):
        for p in peers:
            copy = pltpu.make_async_remote_copy(
                src_ref=ref,
                dst_ref=audio.at[kind, my_audio],
                send_sem=audio_send.at[kind, p],
                recv_sem=audio_recv.at[kind, me],
                device_id={"seq": p},
                device_id_type=MESH,
            )
            copy.start()
            sends.append(copy)
    for h in range(1, share):
        send_heads(h)

    weight_copies = []
    for h in range(share):
        for p in range(seq):
            copy = pltpu.make_async_copy(
                weight.at[pl.ds((p * share + h) * HD, HD)],
                weight_v.at[h, pl.ds(p * HD, HD)],
                weight_sem.at[h, p],
            )
            copy.start()
            weight_copies.append(copy)

    def wait_from(src, dst, send_sem, recv_sem, p):
        pltpu.make_async_remote_copy(
            src_ref=src,
            dst_ref=dst,
            send_sem=send_sem,
            recv_sem=recv_sem,
            device_id={"seq": p},
            device_id_type=MESH,
        ).wait_recv()

    def rows_of(p):
        return pl.ds(pl.multiple_of(p * rows, rows), rows)

    def audio_rows_of(p):
        return pl.ds(pl.multiple_of(p * audio_rows, audio_rows), audio_rows)

    def attend_head(h):
        for kind in range(3):
            local_copies[h * 3 + kind].wait()
        for kind in range(3):
            for p in peers:
                wait_from(
                    vk.at[:, head_cols(p, h)],
                    qkv.at[kind, h, rows_of(p)],
                    qkv_send.at[kind, h, p],
                    qkv_recv.at[kind, h, p],
                    p,
                )
        keyset, values = qkv[0, h], qkv[1, h]
        for p in peers + [me]:
            _, row_sum, numerator = softmax_parts(qkv[2, h, rows_of(p)], keyset, values)
            result = (numerator / row_sum).astype(jnp.bfloat16)
            if p is me:
                gathered[h, me] = result
            else:
                heads_out[h, p] = result
                copy = pltpu.make_async_remote_copy(
                    src_ref=heads_out.at[h, p],
                    dst_ref=gathered.at[h, me],
                    send_sem=out_send.at[h, p],
                    recv_sem=out_recv.at[h, me],
                    device_id={"seq": p},
                    device_id_type=MESH,
                )
                copy.start()
                sends.append(copy)

    def cross_parts():
        for i in range(3):
            loads[i].wait()
        for kind in range(3):
            audio_copies[kind].wait()
            for p in peers:
                wait_from(
                    ak,
                    audio.at[kind, audio_rows_of(p)],
                    audio_send.at[kind, p],
                    audio_recv.at[kind, p],
                    p,
                )
        lane = lax.broadcasted_iota(jnp.int32, (seq * audio_rows, HD), 1)
        held = jnp.zeros((seq * audio_rows, HD), jnp.float32)
        for c in range(cross_heads):
            cols = slice(c * HD, (c + 1) * HD)
            highest, row_sum, numerator = softmax_parts(audio[2, :, cols], ck_v[:, cols], cv_v[:, cols])
            held = jnp.where(lane == c, highest, held)
            held = jnp.where(lane == cross_heads + c, row_sum, held)
            partial[:, cols] = numerator.astype(jnp.bfloat16)
        stats[...] = held
        for p in peers:
            for src, dst, s_sem, r_sem in (
                (partial, partial_in, part_send, part_recv),
                (stats, stats_in, stat_send, stat_recv),
            ):
                copy = pltpu.make_async_remote_copy(
                    src_ref=src.at[audio_rows_of(p)],
                    dst_ref=dst.at[me],
                    send_sem=s_sem.at[p],
                    recv_sem=r_sem.at[me],
                    device_id={"seq": p},
                    device_id_type=MESH,
                )
                copy.start()
                sends.append(copy)
        for c in range(cross_heads):
            cols = slice(c * HD, (c + 1) * HD)
            _, row_sum, numerator = softmax_parts(cq_v[:, cols], audio[0, :, cols], audio[1, :, cols])
            vcross_ref[:, cols] = (numerator / row_sum).astype(jnp.bfloat16)

    def cross_finish():
        for p in peers:
            wait_from(partial.at[audio_rows_of(p)], partial_in.at[p], part_send.at[p], part_recv.at[p], p)
            wait_from(stats.at[audio_rows_of(p)], stats_in.at[p], stat_send.at[p], stat_recv.at[p], p)
        held = [stats[my_audio, :]] + [stats_in[p] for p in peers]
        for c in range(cross_heads):
            cols = slice(c * HD, (c + 1) * HD)
            parts = [partial[my_audio, cols]] + [partial_in[p, :, cols] for p in peers]
            tops = [s[:, c : c + 1] for s in held]
            sums = [s[:, cross_heads + c : cross_heads + c + 1] for s in held]
            highest = functools.reduce(jnp.maximum, tops)
            factors = [jnp.exp(t - highest) for t in tops]
            row_sum = sum(f * s for f, s in zip(factors, sums))
            numerator = sum(f * n.astype(jnp.float32) for f, n in zip(factors, parts))
            across_ref[:, cols] = (numerator / row_sum).astype(jnp.bfloat16)

    def wait_heads(h):
        for p in peers:
            wait_from(heads_out.at[h, p], gathered.at[h, p], out_send.at[h, p], out_recv.at[h, p], p)
        for p in range(seq):
            weight_copies[h * seq + p].wait()
        return jnp.concatenate([gathered[h, p] for p in range(seq)], axis=1)

    def product(attended, h, target, j):
        cols = pl.ds(pl.multiple_of(target * width + j * WIDE, WIDE), WIDE)
        return jnp.dot(attended, weight_v[h, :, cols], preferred_element_type=jnp.float32)

    attend_head(0)
    cross_parts()
    for h in range(1, share):
        attend_head(h)
    cross_finish()
    loads[3].wait()

    slots = [(d, side) for d in list(range(1, chips)) + [0] for side in range(2)]

    def owner_of(d, side):
        return far_chips[d] * 2 + (core if side else 1 - core)

    for h in range(share - 1):
        attended = wait_heads(h)
        for d, side in slots:
            for j in range(pieces):
                value = product(attended, h, owner_of(d, side), j)
                if h:
                    value = value + total[d, side, j]
                total[d, side, j] = value
    last = share - 1
    attended = wait_heads(last)

    def final(d, side, j):
        value = product(attended, last, owner_of(d, side), j)
        if last:
            value = value + total[d, side, j]
        return value

    def pair_copy(d, j):
        return pltpu.make_async_remote_copy(
            src_ref=pair_out.at[d, j],
            dst_ref=pair_in.at[d, j],
            send_sem=pair_send.at[d, j],
            recv_sem=pair_recv.at[d, j],
            device_id={"tensor": sibling},
            device_id_type=MESH,
        )

    def far_copy(d, j):
        return pltpu.make_async_remote_copy(
            src_ref=far_out.at[d - 1, j],
            dst_ref=far_in.at[d - 1, j],
            send_sem=far_send.at[d - 1, j],
            recv_sem=far_recv.at[d - 1, j],
            device_id={"tensor": far_chips[d] * 2 + core},
            device_id_type=MESH,
        )

    def send_pair(d, j):
        pair_out[d, j] = final(d, 0, j).astype(jnp.bfloat16)
        copy = pair_copy(d, j)
        copy.start()
        sends.append(copy)

    def send_far(d, j, value):
        pair_copy(d, j).wait_recv()
        far_out[d - 1, j] = (value + pair_in[d, j].astype(jnp.float32)).astype(jnp.bfloat16)
        copy = far_copy(d, j)
        copy.start()
        sends.append(copy)

    steps = [(d, j) for d in range(1, chips) for j in range(pieces)]
    for d, j in steps:
        send_pair(d, j)
    for d, j in steps:
        send_far(d, j, final(d, 1, j))
    for j in range(pieces):
        send_pair(0, j)
    for j in range(pieces):
        total[0, 1, j] = final(0, 1, j) + stream_v[:, j * WIDE : (j + 1) * WIDE].astype(jnp.float32)
    for j in range(pieces):
        pair_copy(0, j).wait_recv()
        value = total[0, 1, j] + pair_in[0, j].astype(jnp.float32)
        for d in range(1, chips):
            far_copy(d, j).wait_recv()
            value = value + far_in[d - 1, j].astype(jnp.float32)
        next_ref[:, j * WIDE : (j + 1) * WIDE] = value.astype(jnp.bfloat16)
    for copy in sends:
        copy.wait_send()


def fused(seq, tensor, *operands):
    vq, vk, vv, vs, weight, cq, ak, av, aq, ck, cv = operands
    rows, features = vq.shape
    share = features // HD // seq
    audio_rows, cross_width = aq.shape
    chips = tensor // 2
    width = weight.shape[1] // tensor
    pieces = width // WIDE
    bf16, f32, dma = jnp.bfloat16, jnp.float32, pltpu.SemaphoreType.DMA
    return pl.pallas_call(
        functools.partial(block_kernel, seq, tensor),
        out_shape=(
            jax.ShapeDtypeStruct(vs.shape, bf16),
            jax.ShapeDtypeStruct(cq.shape, bf16),
            jax.ShapeDtypeStruct(aq.shape, bf16),
        ),
        in_specs=[pl.BlockSpec(memory_space=pl.ANY)] * 11,
        out_specs=tuple([pl.BlockSpec(memory_space=pltpu.VMEM)] * 3),
        scratch_shapes=[
            pltpu.VMEM((3, share, seq * rows, HD), bf16),
            pltpu.VMEM((share, seq, rows, HD), bf16),
            pltpu.VMEM((share, seq, rows, HD), bf16),
            pltpu.VMEM((3, seq * audio_rows, cross_width), bf16),
            pltpu.VMEM((seq * audio_rows, cross_width), bf16),
            pltpu.VMEM((seq * audio_rows, HD), f32),
            pltpu.VMEM((seq, audio_rows, cross_width), bf16),
            pltpu.VMEM((seq, audio_rows, HD), f32),
            pltpu.VMEM(cq.shape, bf16),
            pltpu.VMEM(ck.shape, bf16),
            pltpu.VMEM(cv.shape, bf16),
            pltpu.VMEM(vs.shape, bf16),
            pltpu.VMEM((share, seq * HD, weight.shape[1]), bf16),
            pltpu.VMEM((chips, 2, pieces, rows, WIDE), f32),
            pltpu.VMEM((chips, pieces, rows, WIDE), bf16),
            pltpu.VMEM((chips, pieces, rows, WIDE), bf16),
            pltpu.VMEM((max(chips - 1, 1), pieces, rows, WIDE), bf16),
            pltpu.VMEM((max(chips - 1, 1), pieces, rows, WIDE), bf16),
            dma((3, share, seq)),
            dma((3, share, seq)),
            dma((3, share)),
            dma((share, seq)),
            dma((share, seq)),
            dma((3, seq)),
            dma((3, seq)),
            dma((3,)),
            dma((seq,)),
            dma((seq,)),
            dma((seq,)),
            dma((seq,)),
            dma((4,)),
            dma((share, seq)),
            dma((chips, pieces)),
            dma((chips, pieces)),
            dma((max(chips - 1, 1), pieces)),
            dma((max(chips - 1, 1), pieces)),
        ],
        compiler_params=pltpu.CompilerParams(
            collective_id=0, has_side_effects=True, vmem_limit_bytes=60000000
        ),
    )(*operands)


def fits(mesh, operands):
    seq, tensor = mesh.shape["seq"], mesh.shape["tensor"]
    vq, weight, cq, aq = operands[0], operands[4], operands[5], operands[8]
    return (
        seq > 1
        and (vq.shape[1] // HD) % seq == 0
        and tensor % 2 == 0
        and (weight.shape[1] // tensor) % WIDE == 0
        and aq.shape[0] % 16 == 0
        and vq.shape[0] % 16 == 0
        and 2 * (cq.shape[1] // HD) <= HD
        and weight.size * 2 <= 16 * 2**20
        and vq.shape[0] <= 256
        and seq <= 8
    )


def solution(mesh):
    def step(*operands):
        if fits(mesh, operands):
            return fused(mesh.shape["seq"], mesh.shape["tensor"], *operands)
        return local(*operands)

    in_specs = (
        P(("groups", "seq"), "tensor"),
        P(("groups", "seq"), "tensor"),
        P(("groups", "seq"), "tensor"),
        P(("groups", "seq"), "tensor"),
        P("tensor", None),
        P(("groups", "seq"), "tensor"),
        P(("groups", "seq"), "tensor"),
        P(("groups", "seq"), "tensor"),
        P(("groups", "seq"), "tensor"),
        P(("groups", "seq"), "tensor"),
        P(("groups", "seq"), "tensor"),
    )
    out_specs = (
        P(("groups", "seq"), "tensor"),
        P(("groups", "seq"), "tensor"),
        P(("groups", "seq"), "tensor"),
    )
    return jax.shard_map(step, mesh=mesh, in_specs=in_specs, out_specs=out_specs, check_vma=False)
```

```python
import functools
import math

import jax
import jax.numpy as jnp
from jax import lax
from jax.experimental import pallas as pl
from jax.experimental.pallas import tpu as pltpu
from jax.sharding import PartitionSpec as P

HD = 128


def blank_state(query_rows, head_count):
    return (
        jnp.full((head_count, query_rows), -1e30, jnp.float32),
        jnp.zeros((head_count, query_rows), jnp.float32),
        jnp.zeros((head_count, query_rows, HD), jnp.float32),
    )


def absorb(carried, queries, keyset, values, head_count):
    running, row_sum, numerator = carried
    query_rows = queries.shape[0]
    key_rows = keyset.shape[0]
    factor = 1.0 / math.sqrt(HD)
    query_heads = queries.reshape(query_rows, head_count, HD)
    for offset in range(0, key_rows, 1024):
        width_keys = min(1024, key_rows - offset)
        key_block = keyset[offset : offset + width_keys].reshape(width_keys, head_count, HD)
        value_block = values[offset : offset + width_keys].reshape(width_keys, head_count, HD)
        scores = (
            jnp.einsum("qhd,khd->hqk", query_heads, key_block, preferred_element_type=jnp.float32)
            * factor
        )
        highest = jnp.maximum(running, jnp.max(scores, axis=2))
        raised = jnp.exp(scores - highest[:, :, None])
        shrink = jnp.exp(running - highest)
        row_sum = row_sum * shrink + jnp.sum(raised, axis=2)
        numerator = numerator * shrink[:, :, None] + jnp.einsum(
            "hqk,khd->hqd",
            raised.astype(jnp.bfloat16),
            value_block,
            preferred_element_type=jnp.float32,
        )
        running = highest
    return (running, row_sum, numerator)


def finish(carried, head_count):
    running, row_sum, numerator = carried
    result = numerator / row_sum[:, :, None]
    return result.transpose(1, 0, 2).reshape(result.shape[1], head_count * HD).astype(jnp.bfloat16)


def local(
    video_query,
    video_key,
    video_value,
    video_stream,
    out_weight,
    cross_query,
    audio_key,
    audio_value,
    audio_query,
    cross_key,
    cross_value,
):
    local_heads = video_query.shape[1] // HD
    query_rows = video_query.shape[0]
    pieces = (
        lax.all_gather(video_key, "seq", axis=0, tiled=True),
        lax.all_gather(video_value, "seq", axis=0, tiled=True),
    )
    carried_video = absorb(
        blank_state(query_rows, local_heads), video_query, pieces[0], pieces[1], local_heads
    )
    attended = finish(carried_video, local_heads)
    projected = jnp.dot(attended, out_weight, preferred_element_type=jnp.float32)
    summed = lax.psum_scatter(
        projected.astype(jnp.bfloat16), "tensor", scatter_dimension=1, tiled=True
    ).astype(jnp.float32)
    video_next = (video_stream.astype(jnp.float32) + summed).astype(jnp.bfloat16)
    cross_heads = cross_query.shape[1] // HD
    every_key, every_value = (
        lax.all_gather(audio_key, "seq", axis=0, tiled=True),
        lax.all_gather(audio_value, "seq", axis=0, tiled=True),
    )
    carried_audio = absorb(
        blank_state(cross_query.shape[0], cross_heads),
        cross_query,
        every_key,
        every_value,
        cross_heads,
    )
    video_cross = finish(carried_audio, cross_heads)
    pieces = (
        lax.all_gather(cross_key, "seq", axis=0, tiled=True),
        lax.all_gather(cross_value, "seq", axis=0, tiled=True),
    )
    carried_cross = absorb(
        blank_state(audio_query.shape[0], cross_heads),
        audio_query,
        pieces[0],
        pieces[1],
        cross_heads,
    )
    audio_cross = finish(carried_cross, cross_heads)
    return (video_next, video_cross, audio_cross)


MESH = pl.DeviceIdType.MESH
NT = (((1,), (1,)), ((), ()))
WIDE = 256
FIRST = 3


def softmax_parts(queries, keyset, values):
    scores = lax.dot_general(queries, keyset, NT, preferred_element_type=jnp.float32) * (
        1.0 / math.sqrt(HD)
    )
    highest = jnp.max(scores, axis=1, keepdims=True)
    raised = jnp.exp(scores - highest)
    row_sum = jnp.sum(raised, axis=1, keepdims=True)
    numerator = jnp.dot(raised.astype(jnp.bfloat16), values, preferred_element_type=jnp.float32)
    return highest, row_sum, numerator


def block_kernel(
    seq,
    tensor,
    vq,
    vk,
    vv,
    vs,
    weight,
    cq,
    ak,
    av,
    aq,
    ck,
    cv,
    next_ref,
    vcross_ref,
    across_ref,
    qkv,
    heads_out,
    gathered,
    audio,
    partial,
    stats,
    partial_in,
    stats_in,
    cq_v,
    ck_v,
    cv_v,
    stream_v,
    weight_v,
    kept,
    pair_out,
    pair_in,
    far_out,
    far_in,
    kv_send,
    kv_recv,
    q_send,
    q_recv,
    own_sem,
    out_send,
    out_recv,
    audio_send,
    audio_recv,
    audio_own,
    part_send,
    part_recv,
    stat_send,
    stat_recv,
    load_sem,
    weight_sem,
    pair_send,
    pair_recv,
    far_send,
    far_recv,
):
    rows = vq.shape[0]
    share = vq.shape[1] // HD // seq
    cross_heads = cq.shape[1] // HD
    audio_rows = aq.shape[0]
    chips = tensor // 2
    width = next_ref.shape[1]
    pieces = width // WIDE
    cuts = row_cuts(rows)
    me = lax.axis_index("seq")
    place = lax.axis_index("tensor")
    core = lax.rem(place, 2)
    chip = place // 2
    sibling = chip * 2 + (1 - core)
    peers = [lax.rem(me + d, seq) for d in range(1, seq)]
    far_chips = [lax.rem(chip + d, chips) for d in range(chips)]

    my_rows = pl.ds(pl.multiple_of(me * rows, rows), rows)
    my_audio = pl.ds(pl.multiple_of(me * audio_rows, audio_rows), audio_rows)

    def head_cols(owner, h):
        return pl.ds(pl.multiple_of((owner * share + h) * HD, HD), HD)

    local_copies = []
    for h in range(share):
        for kind, ref in enumerate((vk, vv, vq)):
            copy = pltpu.make_async_copy(
                ref.at[:, head_cols(me, h)], qkv.at[kind, h, my_rows], own_sem.at[kind, h]
            )
            copy.start()
            local_copies.append(copy)
    audio_copies = []
    for kind, ref in enumerate((ak, av, aq)):
        copy = pltpu.make_async_copy(ref, audio.at[kind, my_audio], audio_own.at[kind])
        copy.start()
        audio_copies.append(copy)
    loads = []
    for i, (ref, dst) in enumerate(((cq, cq_v), (ck, ck_v), (cv, cv_v), (vs, stream_v))):
        copy = pltpu.make_async_copy(ref, dst, load_sem.at[i])
        copy.start()
        loads.append(copy)

    barrier = pltpu.get_barrier_semaphore()
    for p in peers:
        pl.semaphore_signal(barrier, inc=1, device_id={"seq": p}, device_id_type=MESH)
    pl.semaphore_signal(barrier, inc=1, device_id={"tensor": sibling}, device_id_type=MESH)
    for d in range(1, chips):
        pl.semaphore_signal(
            barrier, inc=1, device_id={"tensor": far_chips[d] * 2 + core}, device_id_type=MESH
        )
    pl.semaphore_wait(barrier, seq - 1 + chips)

    sends = []

    def to_seq(src, dst, send_sem, recv_sem, p):
        return pltpu.make_async_remote_copy(
            src_ref=src,
            dst_ref=dst,
            send_sem=send_sem,
            recv_sem=recv_sem,
            device_id={"seq": p},
            device_id_type=MESH,
        )

    def launch(copy):
        copy.start()
        sends.append(copy)

    def cut_of(p, r):
        start, size = cuts[r]
        return pl.ds(pl.multiple_of(p * rows + start, 16), size)

    def send_queries(r):
        start, size = cuts[r]
        for h in range(share):
            for p in peers:
                launch(
                    to_seq(
                        vq.at[pl.ds(start, size), head_cols(p, h)],
                        qkv.at[2, h, cut_of(me, r)],
                        q_send.at[r, h, p],
                        q_recv.at[r, h, me],
                        p,
                    )
                )

    for h in range(share):
        for kind, ref in enumerate((vk, vv)):
            for p in peers:
                launch(
                    to_seq(
                        ref.at[:, head_cols(p, h)],
                        qkv.at[kind, h, my_rows],
                        kv_send.at[kind, h, p],
                        kv_recv.at[kind, h, me],
                        p,
                    )
                )
    send_queries(0)
    for kind, ref in enumerate((ak, av, aq)):
        for p in peers:
            launch(to_seq(ref, audio.at[kind, my_audio], audio_send.at[kind, p], audio_recv.at[kind, me], p))
    for r in range(1, len(cuts)):
        send_queries(r)

    weight_copy = pltpu.make_async_copy(weight, weight_v, weight_sem)
    weight_copy.start()

    def wait_from(src, dst, send_sem, recv_sem, p):
        to_seq(src, dst, send_sem, recv_sem, p).wait_recv()

    def rows_of(p):
        return pl.ds(pl.multiple_of(p * rows, rows), rows)

    def audio_rows_of(p):
        return pl.ds(pl.multiple_of(p * audio_rows, audio_rows), audio_rows)

    def wait_keys():
        for copy in local_copies:
            copy.wait()
        for h in range(share):
            for kind, ref in enumerate((vk, vv)):
                for p in peers:
                    wait_from(
                        ref.at[:, head_cols(p, h)],
                        qkv.at[kind, h, rows_of(p)],
                        kv_send.at[kind, h, p],
                        kv_recv.at[kind, h, p],
                        p,
                    )

    def attend_rows(r):
        start, size = cuts[r]
        here = pl.ds(start, size)
        for h in range(share):
            keyset, values = qkv[0, h], qkv[1, h]
            for p in peers + [me]:
                if p is not me:
                    wait_from(
                        vq.at[here, head_cols(p, h)],
                        qkv.at[2, h, cut_of(p, r)],
                        q_send.at[r, h, p],
                        q_recv.at[r, h, p],
                        p,
                    )
                _, row_sum, numerator = softmax_parts(qkv[2, h, cut_of(p, r)], keyset, values)
                result = (numerator / row_sum).astype(jnp.bfloat16)
                if p is me:
                    gathered[h, me, here] = result
                else:
                    heads_out[h, p, here] = result
                    launch(
                        to_seq(
                            heads_out.at[h, p, here],
                            gathered.at[h, me, here],
                            out_send.at[r, h, p],
                            out_recv.at[r, h, me],
                            p,
                        )
                    )

    def cross_parts():
        for i in range(3):
            loads[i].wait()
        for kind in range(3):
            audio_copies[kind].wait()
            for p in peers:
                wait_from(
                    ak,
                    audio.at[kind, audio_rows_of(p)],
                    audio_send.at[kind, p],
                    audio_recv.at[kind, p],
                    p,
                )
        lane = lax.broadcasted_iota(jnp.int32, (seq * audio_rows, HD), 1)
        held = jnp.zeros((seq * audio_rows, HD), jnp.float32)
        for c in range(cross_heads):
            cols = slice(c * HD, (c + 1) * HD)
            highest, row_sum, numerator = softmax_parts(audio[2, :, cols], ck_v[:, cols], cv_v[:, cols])
            held = jnp.where(lane == c, highest, held)
            held = jnp.where(lane == cross_heads + c, row_sum, held)
            partial[:, cols] = numerator.astype(jnp.bfloat16)
        stats[...] = held
        for p in peers:
            for src, dst, s_sem, r_sem in (
                (partial, partial_in, part_send, part_recv),
                (stats, stats_in, stat_send, stat_recv),
            ):
                copy = pltpu.make_async_remote_copy(
                    src_ref=src.at[audio_rows_of(p)],
                    dst_ref=dst.at[me],
                    send_sem=s_sem.at[p],
                    recv_sem=r_sem.at[me],
                    device_id={"seq": p},
                    device_id_type=MESH,
                )
                copy.start()
                sends.append(copy)
        for c in range(cross_heads):
            cols = slice(c * HD, (c + 1) * HD)
            _, row_sum, numerator = softmax_parts(cq_v[:, cols], audio[0, :, cols], audio[1, :, cols])
            vcross_ref[:, cols] = (numerator / row_sum).astype(jnp.bfloat16)

    def cross_finish():
        for p in peers:
            wait_from(partial.at[audio_rows_of(p)], partial_in.at[p], part_send.at[p], part_recv.at[p], p)
            wait_from(stats.at[audio_rows_of(p)], stats_in.at[p], stat_send.at[p], stat_recv.at[p], p)
        held = [stats[my_audio, :]] + [stats_in[p] for p in peers]
        for c in range(cross_heads):
            cols = slice(c * HD, (c + 1) * HD)
            parts = [partial[my_audio, cols]] + [partial_in[p, :, cols] for p in peers]
            tops = [s[:, c : c + 1] for s in held]
            sums = [s[:, cross_heads + c : cross_heads + c + 1] for s in held]
            highest = functools.reduce(jnp.maximum, tops)
            factors = [jnp.exp(t - highest) for t in tops]
            row_sum = sum(f * s for f, s in zip(factors, sums))
            numerator = sum(f * n.astype(jnp.float32) for f, n in zip(factors, parts))
            across_ref[:, cols] = (numerator / row_sum).astype(jnp.bfloat16)

    def wait_heads(r):
        here = pl.ds(*cuts[r])
        for h in range(share):
            for p in peers:
                wait_from(
                    heads_out.at[h, p, here],
                    gathered.at[h, p, here],
                    out_send.at[r, h, p],
                    out_recv.at[r, h, p],
                    p,
                )
        return jnp.concatenate(
            [gathered[h, p, here] for p in range(seq) for h in range(share)], axis=1
        )

    def product(attended, d, side, j):
        target = far_chips[d] * 2 + (core if side else 1 - core)
        cols = pl.ds(pl.multiple_of(target * width + j * WIDE, WIDE), WIDE)
        return jnp.dot(attended, weight_v[:, cols], preferred_element_type=jnp.float32)

    def pair_copy(r, d, j):
        here = pl.ds(*cuts[r])
        return pltpu.make_async_remote_copy(
            src_ref=pair_out.at[d, j, here],
            dst_ref=pair_in.at[d, j, here],
            send_sem=pair_send.at[r, d, j],
            recv_sem=pair_recv.at[r, d, j],
            device_id={"tensor": sibling},
            device_id_type=MESH,
        )

    def far_copy(r, d, j):
        here = pl.ds(*cuts[r])
        return pltpu.make_async_remote_copy(
            src_ref=far_out.at[d - 1, j, here],
            dst_ref=far_in.at[d - 1, j, here],
            send_sem=far_send.at[r, d - 1, j],
            recv_sem=far_recv.at[r, d - 1, j],
            device_id={"tensor": far_chips[d] * 2 + core},
            device_id_type=MESH,
        )

    def share_rows(r):
        here = pl.ds(*cuts[r])
        attended = wait_heads(r)
        if r == 0:
            weight_copy.wait()
        steps = [(d, j) for d in range(1, chips) for j in range(pieces)]
        for d, j in steps + [(0, j) for j in range(pieces)]:
            pair_out[d, j, here] = product(attended, d, 0, j).astype(jnp.bfloat16)
            launch(pair_copy(r, d, j))
            if d:
                mine = product(attended, d, 1, j)
                pair_copy(r, d, j).wait_recv()
                far_out[d - 1, j, here] = (mine + pair_in[d, j, here].astype(jnp.float32)).astype(
                    jnp.bfloat16
                )
                launch(far_copy(r, d, j))
        for j in range(pieces):
            block = slice(j * WIDE, (j + 1) * WIDE)
            kept[here, block] = product(attended, 0, 1, j) + stream_v[here, block].astype(jnp.float32)

    def close_rows(r):
        here = pl.ds(*cuts[r])
        for j in range(pieces):
            block = slice(j * WIDE, (j + 1) * WIDE)
            pair_copy(r, 0, j).wait_recv()
            value = kept[here, block] + pair_in[0, j, here].astype(jnp.float32)
            for d in range(1, chips):
                far_copy(r, d, j).wait_recv()
                value = value + far_in[d - 1, j, here].astype(jnp.float32)
            next_ref[here, block] = value.astype(jnp.bfloat16)

    wait_keys()
    attend_rows(0)
    cross_parts()
    for r in range(1, len(cuts)):
        attend_rows(r)
    loads[3].wait()
    for r in range(len(cuts)):
        share_rows(r)
        if r == 0:
            cross_finish()
    for r in range(len(cuts)):
        close_rows(r)
    for copy in sends:
        copy.wait_send()


def row_cuts(rows):
    first = max(rows * FIRST // 4 // 16 * 16, 16)
    return [(0, first), (first, rows - first)] if first < rows else [(0, rows)]


def write_out(*refs):
    half = len(refs) // 2
    for src, dst in zip(refs[:half], refs[half:]):
        dst[...] = src[...]


def fused(seq, tensor, *operands):
    vq, vk, vv, vs, weight, cq, ak, av, aq, ck, cv = operands
    rows, features = vq.shape
    share = features // HD // seq
    audio_rows, cross_width = aq.shape
    chips = tensor // 2
    width = weight.shape[1] // tensor
    pieces = width // WIDE
    groups = len(row_cuts(rows))
    bf16, f32, dma = jnp.bfloat16, jnp.float32, pltpu.SemaphoreType.DMA
    shapes = tuple(jax.ShapeDtypeStruct(x.shape, bf16) for x in (vs, cq, aq))
    whole = pl.BlockSpec(memory_space=pltpu.VMEM)
    results = pl.pallas_call(
        functools.partial(block_kernel, seq, tensor),
        out_shape=tuple(pltpu.VMEM(x.shape, bf16) for x in (vs, cq, aq)),
        in_specs=[pl.BlockSpec(memory_space=pltpu.HBM)] * 11,
        out_specs=(whole,) * 3,
        scratch_shapes=[
            pltpu.VMEM((3, share, seq * rows, HD), bf16),
            pltpu.VMEM((share, seq, rows, HD), bf16),
            pltpu.VMEM((share, seq, rows, HD), bf16),
            pltpu.VMEM((3, seq * audio_rows, cross_width), bf16),
            pltpu.VMEM((seq * audio_rows, cross_width), bf16),
            pltpu.VMEM((seq * audio_rows, HD), f32),
            pltpu.VMEM((seq, audio_rows, cross_width), bf16),
            pltpu.VMEM((seq, audio_rows, HD), f32),
            pltpu.VMEM(cq.shape, bf16),
            pltpu.VMEM(ck.shape, bf16),
            pltpu.VMEM(cv.shape, bf16),
            pltpu.VMEM(vs.shape, bf16),
            pltpu.VMEM(weight.shape, bf16),
            pltpu.VMEM(vs.shape, f32),
            pltpu.VMEM((chips, pieces, rows, WIDE), bf16),
            pltpu.VMEM((chips, pieces, rows, WIDE), bf16),
            pltpu.VMEM((max(chips - 1, 1), pieces, rows, WIDE), bf16),
            pltpu.VMEM((max(chips - 1, 1), pieces, rows, WIDE), bf16),
            dma((2, share, seq)),
            dma((2, share, seq)),
            dma((groups, share, seq)),
            dma((groups, share, seq)),
            dma((3, share)),
            dma((groups, share, seq)),
            dma((groups, share, seq)),
            dma((3, seq)),
            dma((3, seq)),
            dma((3,)),
            dma((seq,)),
            dma((seq,)),
            dma((seq,)),
            dma((seq,)),
            dma((4,)),
            dma(()),
            dma((groups, chips, pieces)),
            dma((groups, chips, pieces)),
            dma((groups, max(chips - 1, 1), pieces)),
            dma((groups, max(chips - 1, 1), pieces)),
        ],
        compiler_params=pltpu.CompilerParams(
            collective_id=0, has_side_effects=True, vmem_limit_bytes=60000000
        ),
    )(*operands)
    return pl.pallas_call(
        write_out,
        out_shape=shapes,
        in_specs=[whole] * 3,
        out_specs=(whole,) * 3,
        compiler_params=pltpu.CompilerParams(vmem_limit_bytes=8 * 2**20),
    )(*results)


def fits(mesh, operands):
    seq, tensor = mesh.shape["seq"], mesh.shape["tensor"]
    vq, weight, cq, aq = operands[0], operands[4], operands[5], operands[8]
    return (
        seq > 1
        and (vq.shape[1] // HD) % seq == 0
        and tensor % 2 == 0
        and (weight.shape[1] // tensor) % WIDE == 0
        and aq.shape[0] % 16 == 0
        and vq.shape[0] % 16 == 0
        and 2 * (cq.shape[1] // HD) <= HD
        and weight.size * 2 <= 10 * 2**20
        and vq.shape[0] <= 128
        and seq <= 8
    )


def solution(mesh):
    def step(*operands):
        if fits(mesh, operands):
            return fused(mesh.shape["seq"], mesh.shape["tensor"], *operands)
        return local(*operands)

    in_specs = (
        P(("groups", "seq"), "tensor"),
        P(("groups", "seq"), "tensor"),
        P(("groups", "seq"), "tensor"),
        P(("groups", "seq"), "tensor"),
        P("tensor", None),
        P(("groups", "seq"), "tensor"),
        P(("groups", "seq"), "tensor"),
        P(("groups", "seq"), "tensor"),
        P(("groups", "seq"), "tensor"),
        P(("groups", "seq"), "tensor"),
        P(("groups", "seq"), "tensor"),
    )
    out_specs = (
        P(("groups", "seq"), "tensor"),
        P(("groups", "seq"), "tensor"),
        P(("groups", "seq"), "tensor"),
    )
    return jax.shard_map(step, mesh=mesh, in_specs=in_specs, out_specs=out_specs, check_vma=False)
```

```python
import functools
import math

import jax
import jax.numpy as jnp
from jax import lax
from jax.experimental import pallas as pl
from jax.experimental.pallas import tpu as pltpu
from jax.sharding import PartitionSpec as P

HD = 128


def blank_state(query_rows, head_count):
    return (
        jnp.full((head_count, query_rows), -1e30, jnp.float32),
        jnp.zeros((head_count, query_rows), jnp.float32),
        jnp.zeros((head_count, query_rows, HD), jnp.float32),
    )


def absorb(carried, queries, keyset, values, head_count):
    running, row_sum, numerator = carried
    query_rows = queries.shape[0]
    key_rows = keyset.shape[0]
    factor = 1.0 / math.sqrt(HD)
    query_heads = queries.reshape(query_rows, head_count, HD)
    for offset in range(0, key_rows, 1024):
        width_keys = min(1024, key_rows - offset)
        key_block = keyset[offset : offset + width_keys].reshape(width_keys, head_count, HD)
        value_block = values[offset : offset + width_keys].reshape(width_keys, head_count, HD)
        scores = (
            jnp.einsum("qhd,khd->hqk", query_heads, key_block, preferred_element_type=jnp.float32)
            * factor
        )
        highest = jnp.maximum(running, jnp.max(scores, axis=2))
        raised = jnp.exp(scores - highest[:, :, None])
        shrink = jnp.exp(running - highest)
        row_sum = row_sum * shrink + jnp.sum(raised, axis=2)
        numerator = numerator * shrink[:, :, None] + jnp.einsum(
            "hqk,khd->hqd",
            raised.astype(jnp.bfloat16),
            value_block,
            preferred_element_type=jnp.float32,
        )
        running = highest
    return (running, row_sum, numerator)


def finish(carried, head_count):
    running, row_sum, numerator = carried
    result = numerator / row_sum[:, :, None]
    return result.transpose(1, 0, 2).reshape(result.shape[1], head_count * HD).astype(jnp.bfloat16)


def local(
    video_query,
    video_key,
    video_value,
    video_stream,
    out_weight,
    cross_query,
    audio_key,
    audio_value,
    audio_query,
    cross_key,
    cross_value,
):
    local_heads = video_query.shape[1] // HD
    query_rows = video_query.shape[0]
    pieces = (
        lax.all_gather(video_key, "seq", axis=0, tiled=True),
        lax.all_gather(video_value, "seq", axis=0, tiled=True),
    )
    carried_video = absorb(
        blank_state(query_rows, local_heads), video_query, pieces[0], pieces[1], local_heads
    )
    attended = finish(carried_video, local_heads)
    projected = jnp.dot(attended, out_weight, preferred_element_type=jnp.float32)
    summed = lax.psum_scatter(
        projected.astype(jnp.bfloat16), "tensor", scatter_dimension=1, tiled=True
    ).astype(jnp.float32)
    video_next = (video_stream.astype(jnp.float32) + summed).astype(jnp.bfloat16)
    cross_heads = cross_query.shape[1] // HD
    every_key, every_value = (
        lax.all_gather(audio_key, "seq", axis=0, tiled=True),
        lax.all_gather(audio_value, "seq", axis=0, tiled=True),
    )
    carried_audio = absorb(
        blank_state(cross_query.shape[0], cross_heads),
        cross_query,
        every_key,
        every_value,
        cross_heads,
    )
    video_cross = finish(carried_audio, cross_heads)
    pieces = (
        lax.all_gather(cross_key, "seq", axis=0, tiled=True),
        lax.all_gather(cross_value, "seq", axis=0, tiled=True),
    )
    carried_cross = absorb(
        blank_state(audio_query.shape[0], cross_heads),
        audio_query,
        pieces[0],
        pieces[1],
        cross_heads,
    )
    audio_cross = finish(carried_cross, cross_heads)
    return (video_next, video_cross, audio_cross)


MESH = pl.DeviceIdType.MESH
NT = (((1,), (1,)), ((), ()))
WIDE = 512
FIRST = 3


def softmax_parts(queries, keyset, values):
    scores = lax.dot_general(queries, keyset, NT, preferred_element_type=jnp.float32) * (
        1.0 / math.sqrt(HD)
    )
    highest = jnp.max(scores, axis=1, keepdims=True)
    raised = jnp.exp(scores - highest)
    row_sum = jnp.sum(raised, axis=1, keepdims=True)
    numerator = jnp.dot(raised.astype(jnp.bfloat16), values, preferred_element_type=jnp.float32)
    return highest, row_sum, numerator


def block_kernel(
    seq,
    tensor,
    vq,
    vk,
    vv,
    vs,
    weight,
    cq,
    ak,
    av,
    aq,
    ck,
    cv,
    next_ref,
    vcross_ref,
    across_ref,
    qkv,
    heads_out,
    gathered,
    audio,
    partial,
    stats,
    partial_in,
    stats_in,
    cq_v,
    ck_v,
    cv_v,
    stream_v,
    weight_v,
    kept,
    pair_out,
    pair_in,
    far_out,
    far_in,
    kv_send,
    kv_recv,
    q_send,
    q_recv,
    own_sem,
    out_send,
    out_recv,
    audio_send,
    audio_recv,
    audio_own,
    part_send,
    part_recv,
    stat_send,
    stat_recv,
    load_sem,
    weight_sem,
    pair_send,
    pair_recv,
    far_send,
    far_recv,
):
    rows = vq.shape[0]
    share = vq.shape[1] // HD // seq
    cross_heads = cq.shape[1] // HD
    audio_rows = aq.shape[0]
    chips = tensor // 2
    width = next_ref.shape[1]
    pieces = width // WIDE
    cuts = row_cuts(rows)
    me = lax.axis_index("seq")
    place = lax.axis_index("tensor")
    core = lax.rem(place, 2)
    chip = place // 2
    sibling = chip * 2 + (1 - core)
    peers = [lax.rem(me + d, seq) for d in range(1, seq)]
    far_chips = [lax.rem(chip + d, chips) for d in range(chips)]

    my_rows = pl.ds(pl.multiple_of(me * rows, rows), rows)
    my_audio = pl.ds(pl.multiple_of(me * audio_rows, audio_rows), audio_rows)

    def head_cols(owner, h):
        return pl.ds(pl.multiple_of((owner * share + h) * HD, HD), HD)

    local_copies = []
    for h in range(share):
        for kind, ref in enumerate((vk, vv, vq)):
            copy = pltpu.make_async_copy(
                ref.at[:, head_cols(me, h)], qkv.at[kind, h, my_rows], own_sem.at[kind, h]
            )
            copy.start()
            local_copies.append(copy)
    audio_copies = []
    for kind, ref in enumerate((ak, av, aq)):
        copy = pltpu.make_async_copy(ref, audio.at[kind, my_audio], audio_own.at[kind])
        copy.start()
        audio_copies.append(copy)
    loads = []
    for i, (ref, dst) in enumerate(((cq, cq_v), (ck, ck_v), (cv, cv_v), (vs, stream_v))):
        copy = pltpu.make_async_copy(ref, dst, load_sem.at[i])
        copy.start()
        loads.append(copy)

    barrier = pltpu.get_barrier_semaphore()
    for p in peers:
        pl.semaphore_signal(barrier, inc=1, device_id={"seq": p}, device_id_type=MESH)
    pl.semaphore_signal(barrier, inc=1, device_id={"tensor": sibling}, device_id_type=MESH)
    for d in range(1, chips):
        pl.semaphore_signal(
            barrier, inc=1, device_id={"tensor": far_chips[d] * 2 + core}, device_id_type=MESH
        )
    pl.semaphore_wait(barrier, seq - 1 + chips)

    sends = []

    def to_seq(src, dst, send_sem, recv_sem, p):
        return pltpu.make_async_remote_copy(
            src_ref=src,
            dst_ref=dst,
            send_sem=send_sem,
            recv_sem=recv_sem,
            device_id={"seq": p},
            device_id_type=MESH,
        )

    def launch(copy):
        copy.start()
        sends.append(copy)

    def cut_of(p, r):
        start, size = cuts[r]
        return pl.ds(pl.multiple_of(p * rows + start, 16), size)

    def send_queries(r):
        start, size = cuts[r]
        for h in range(share):
            for p in peers:
                launch(
                    to_seq(
                        vq.at[pl.ds(start, size), head_cols(p, h)],
                        qkv.at[2, h, cut_of(me, r)],
                        q_send.at[r, h, p],
                        q_recv.at[r, h, me],
                        p,
                    )
                )

    def rows_of(p):
        return pl.ds(pl.multiple_of(p * rows, rows), rows)

    def audio_rows_of(p):
        return pl.ds(pl.multiple_of(p * audio_rows, audio_rows), audio_rows)

    def audio_hop(step, way):
        shard = lax.rem(me - way * step + seq, seq)
        here = audio_rows_of(shard)
        return to_seq(
            audio.at[:, here],
            audio.at[:, here],
            audio_send.at[step, (way + 1) // 2],
            audio_recv.at[shard],
            lax.rem(me + way + seq, seq),
        )

    def on_line(step, way):
        source, target = me - way * step, me + way
        return (source >= 0) & (source < seq) & (target >= 0) & (target < seq)

    def pass_audio(step):
        for way in (1, -1):

            @pl.when(on_line(step, way))
            def _():
                copy = audio_hop(step, way)
                if step:
                    copy.wait_recv()
                copy.start()

    def end_audio():
        for step in range(1, seq):
            for way in (1, -1):
                source, target = me - way * step, me + way
                last = (target < 0) | (target >= seq)

                @pl.when((source >= 0) & (source < seq) & last)
                def _():
                    audio_hop(step, way).wait_recv()

    for copy in audio_copies:
        copy.wait()
    pass_audio(0)
    for h in range(share):
        for kind, ref in enumerate((vk, vv)):
            for p in peers:
                launch(
                    to_seq(
                        ref.at[:, head_cols(p, h)],
                        qkv.at[kind, h, my_rows],
                        kv_send.at[kind, h, p],
                        kv_recv.at[kind, h, me],
                        p,
                    )
                )
    pass_audio(1)
    send_queries(0)
    for r in range(1, len(cuts)):
        send_queries(r)

    weight_copy = pltpu.make_async_copy(weight, weight_v, weight_sem)
    weight_copy.start()

    def wait_from(src, dst, send_sem, recv_sem, p):
        to_seq(src, dst, send_sem, recv_sem, p).wait_recv()

    def wait_keys():
        for copy in local_copies:
            copy.wait()
        for h in range(share):
            for kind, ref in enumerate((vk, vv)):
                for p in peers:
                    wait_from(
                        ref.at[:, head_cols(p, h)],
                        qkv.at[kind, h, rows_of(p)],
                        kv_send.at[kind, h, p],
                        kv_recv.at[kind, h, p],
                        p,
                    )

    def attend_rows(r):
        start, size = cuts[r]
        here = pl.ds(start, size)
        for h in range(share):
            keyset, values = qkv[0, h], qkv[1, h]
            for p in peers + [me]:
                if p is not me:
                    wait_from(
                        vq.at[here, head_cols(p, h)],
                        qkv.at[2, h, cut_of(p, r)],
                        q_send.at[r, h, p],
                        q_recv.at[r, h, p],
                        p,
                    )
                _, row_sum, numerator = softmax_parts(qkv[2, h, cut_of(p, r)], keyset, values)
                result = (numerator / row_sum).astype(jnp.bfloat16)
                if p is me:
                    gathered[h, me, here] = result
                else:
                    heads_out[h, p, here] = result
                    launch(
                        to_seq(
                            heads_out.at[h, p, here],
                            gathered.at[h, me, here],
                            out_send.at[r, h, p],
                            out_recv.at[r, h, me],
                            p,
                        )
                    )

    def cross_parts():
        for i in range(3):
            loads[i].wait()
        end_audio()
        lane = lax.broadcasted_iota(jnp.int32, (seq * audio_rows, HD), 1)
        held = jnp.zeros((seq * audio_rows, HD), jnp.float32)
        for c in range(cross_heads):
            cols = slice(c * HD, (c + 1) * HD)
            highest, row_sum, numerator = softmax_parts(audio[2, :, cols], ck_v[:, cols], cv_v[:, cols])
            held = jnp.where(lane == c, highest, held)
            held = jnp.where(lane == cross_heads + c, row_sum, held)
            partial[:, cols] = numerator.astype(jnp.bfloat16)
        stats[...] = held
        for p in peers:
            for src, dst, s_sem, r_sem in (
                (partial, partial_in, part_send, part_recv),
                (stats, stats_in, stat_send, stat_recv),
            ):
                copy = pltpu.make_async_remote_copy(
                    src_ref=src.at[audio_rows_of(p)],
                    dst_ref=dst.at[me],
                    send_sem=s_sem.at[p],
                    recv_sem=r_sem.at[me],
                    device_id={"seq": p},
                    device_id_type=MESH,
                )
                copy.start()
                sends.append(copy)
        for c in range(cross_heads):
            cols = slice(c * HD, (c + 1) * HD)
            _, row_sum, numerator = softmax_parts(cq_v[:, cols], audio[0, :, cols], audio[1, :, cols])
            vcross_ref[:, cols] = (numerator / row_sum).astype(jnp.bfloat16)

    def cross_finish():
        for p in peers:
            wait_from(partial.at[audio_rows_of(p)], partial_in.at[p], part_send.at[p], part_recv.at[p], p)
            wait_from(stats.at[audio_rows_of(p)], stats_in.at[p], stat_send.at[p], stat_recv.at[p], p)
        held = [stats[my_audio, :]] + [stats_in[p] for p in peers]
        for c in range(cross_heads):
            cols = slice(c * HD, (c + 1) * HD)
            parts = [partial[my_audio, cols]] + [partial_in[p, :, cols] for p in peers]
            tops = [s[:, c : c + 1] for s in held]
            sums = [s[:, cross_heads + c : cross_heads + c + 1] for s in held]
            highest = functools.reduce(jnp.maximum, tops)
            factors = [jnp.exp(t - highest) for t in tops]
            row_sum = sum(f * s for f, s in zip(factors, sums))
            numerator = sum(f * n.astype(jnp.float32) for f, n in zip(factors, parts))
            across_ref[:, cols] = (numerator / row_sum).astype(jnp.bfloat16)

    def wait_heads(r):
        here = pl.ds(*cuts[r])
        for h in range(share):
            for p in peers:
                wait_from(
                    heads_out.at[h, p, here],
                    gathered.at[h, p, here],
                    out_send.at[r, h, p],
                    out_recv.at[r, h, p],
                    p,
                )
        return jnp.concatenate(
            [gathered[h, p, here] for p in range(seq) for h in range(share)], axis=1
        )

    def product(attended, d, side, j):
        target = far_chips[d] * 2 + (core if side else 1 - core)
        cols = pl.ds(pl.multiple_of(target * width + j * WIDE, WIDE), WIDE)
        return jnp.dot(attended, weight_v[:, cols], preferred_element_type=jnp.float32)

    def pair_copy(r, d, j):
        here = pl.ds(*cuts[r])
        return pltpu.make_async_remote_copy(
            src_ref=pair_out.at[d, j, here],
            dst_ref=pair_in.at[d, j, here],
            send_sem=pair_send.at[r, d, j],
            recv_sem=pair_recv.at[r, d, j],
            device_id={"tensor": sibling},
            device_id_type=MESH,
        )

    def far_copy(r, d, j):
        here = pl.ds(*cuts[r])
        return pltpu.make_async_remote_copy(
            src_ref=far_out.at[d - 1, j, here],
            dst_ref=far_in.at[d - 1, j, here],
            send_sem=far_send.at[r, d - 1, j],
            recv_sem=far_recv.at[r, d - 1, j],
            device_id={"tensor": far_chips[d] * 2 + core},
            device_id_type=MESH,
        )

    def share_rows(r):
        here = pl.ds(*cuts[r])
        attended = wait_heads(r)
        if r == 0:
            weight_copy.wait()
        steps = [(d, j) for d in range(1, chips) for j in range(pieces)]
        for d, j in steps:
            pair_out[d, j, here] = product(attended, d, 0, j).astype(jnp.bfloat16)
            launch(pair_copy(r, d, j))
        for d, j in steps:
            mine = product(attended, d, 1, j)
            pair_copy(r, d, j).wait_recv()
            far_out[d - 1, j, here] = (mine + pair_in[d, j, here].astype(jnp.float32)).astype(
                jnp.bfloat16
            )
            launch(far_copy(r, d, j))
        for j in range(pieces):
            pair_out[0, j, here] = product(attended, 0, 0, j).astype(jnp.bfloat16)
            launch(pair_copy(r, 0, j))
        for j in range(pieces):
            block = slice(j * WIDE, (j + 1) * WIDE)
            kept[here, block] = product(attended, 0, 1, j) + stream_v[here, block].astype(jnp.float32)

    def close_rows(r):
        here = pl.ds(*cuts[r])
        for j in range(pieces):
            block = slice(j * WIDE, (j + 1) * WIDE)
            pair_copy(r, 0, j).wait_recv()
            value = kept[here, block] + pair_in[0, j, here].astype(jnp.float32)
            for d in range(1, chips):
                far_copy(r, d, j).wait_recv()
                value = value + far_in[d - 1, j, here].astype(jnp.float32)
            next_ref[here, block] = value.astype(jnp.bfloat16)

    wait_keys()
    for step in range(2, seq - 1):
        pass_audio(step)
    attend_rows(0)
    cross_parts()
    for r in range(1, len(cuts)):
        attend_rows(r)
    loads[3].wait()
    for r in range(len(cuts)):
        share_rows(r)
        if r == 0:
            cross_finish()
    for r in range(len(cuts)):
        close_rows(r)
    for copy in sends:
        copy.wait_send()
    for step in range(seq - 1):
        for way in (1, -1):

            @pl.when(on_line(step, way))
            def _():
                audio_hop(step, way).wait_send()


def row_cuts(rows):
    first = max(rows * FIRST // 4 // 16 * 16, 16)
    return [(0, first), (first, rows - first)] if first < rows else [(0, rows)]


def write_out(*refs):
    half = len(refs) // 2
    for src, dst in zip(refs[:half], refs[half:]):
        dst[...] = src[...]


def fused(seq, tensor, *operands):
    vq, vk, vv, vs, weight, cq, ak, av, aq, ck, cv = operands
    rows, features = vq.shape
    share = features // HD // seq
    audio_rows, cross_width = aq.shape
    chips = tensor // 2
    width = weight.shape[1] // tensor
    pieces = width // WIDE
    groups = len(row_cuts(rows))
    bf16, f32, dma = jnp.bfloat16, jnp.float32, pltpu.SemaphoreType.DMA
    shapes = tuple(jax.ShapeDtypeStruct(x.shape, bf16) for x in (vs, cq, aq))
    whole = pl.BlockSpec(memory_space=pltpu.VMEM)
    results = pl.pallas_call(
        functools.partial(block_kernel, seq, tensor),
        out_shape=tuple(pltpu.VMEM(x.shape, bf16) for x in (vs, cq, aq)),
        in_specs=[pl.BlockSpec(memory_space=pltpu.HBM)] * 11,
        out_specs=(whole,) * 3,
        scratch_shapes=[
            pltpu.VMEM((3, share, seq * rows, HD), bf16),
            pltpu.VMEM((share, seq, rows, HD), bf16),
            pltpu.VMEM((share, seq, rows, HD), bf16),
            pltpu.VMEM((3, seq * audio_rows, cross_width), bf16),
            pltpu.VMEM((seq * audio_rows, cross_width), bf16),
            pltpu.VMEM((seq * audio_rows, HD), f32),
            pltpu.VMEM((seq, audio_rows, cross_width), bf16),
            pltpu.VMEM((seq, audio_rows, HD), f32),
            pltpu.VMEM(cq.shape, bf16),
            pltpu.VMEM(ck.shape, bf16),
            pltpu.VMEM(cv.shape, bf16),
            pltpu.VMEM(vs.shape, bf16),
            pltpu.VMEM(weight.shape, bf16),
            pltpu.VMEM(vs.shape, f32),
            pltpu.VMEM((chips, pieces, rows, WIDE), bf16),
            pltpu.VMEM((chips, pieces, rows, WIDE), bf16),
            pltpu.VMEM((max(chips - 1, 1), pieces, rows, WIDE), bf16),
            pltpu.VMEM((max(chips - 1, 1), pieces, rows, WIDE), bf16),
            dma((2, share, seq)),
            dma((2, share, seq)),
            dma((groups, share, seq)),
            dma((groups, share, seq)),
            dma((3, share)),
            dma((groups, share, seq)),
            dma((groups, share, seq)),
            dma((seq, 2)),
            dma((seq,)),
            dma((3,)),
            dma((seq,)),
            dma((seq,)),
            dma((seq,)),
            dma((seq,)),
            dma((4,)),
            dma(()),
            dma((groups, chips, pieces)),
            dma((groups, chips, pieces)),
            dma((groups, max(chips - 1, 1), pieces)),
            dma((groups, max(chips - 1, 1), pieces)),
        ],
        compiler_params=pltpu.CompilerParams(
            collective_id=0, has_side_effects=True, vmem_limit_bytes=60000000
        ),
    )(*operands)
    return pl.pallas_call(
        write_out,
        out_shape=shapes,
        in_specs=[whole] * 3,
        out_specs=(whole,) * 3,
        compiler_params=pltpu.CompilerParams(vmem_limit_bytes=8 * 2**20),
    )(*results)


def fits(mesh, operands):
    seq, tensor = mesh.shape["seq"], mesh.shape["tensor"]
    vq, weight, cq, aq = operands[0], operands[4], operands[5], operands[8]
    return (
        seq > 1
        and (vq.shape[1] // HD) % seq == 0
        and tensor % 2 == 0
        and (weight.shape[1] // tensor) % WIDE == 0
        and aq.shape[0] % 16 == 0
        and vq.shape[0] % 16 == 0
        and 2 * (cq.shape[1] // HD) <= HD
        and weight.size * 2 <= 10 * 2**20
        and vq.shape[0] <= 128
        and seq <= 8
    )


def solution(mesh):
    def step(*operands):
        if fits(mesh, operands):
            return fused(mesh.shape["seq"], mesh.shape["tensor"], *operands)
        return local(*operands)

    in_specs = (
        P(("groups", "seq"), "tensor"),
        P(("groups", "seq"), "tensor"),
        P(("groups", "seq"), "tensor"),
        P(("groups", "seq"), "tensor"),
        P("tensor", None),
        P(("groups", "seq"), "tensor"),
        P(("groups", "seq"), "tensor"),
        P(("groups", "seq"), "tensor"),
        P(("groups", "seq"), "tensor"),
        P(("groups", "seq"), "tensor"),
        P(("groups", "seq"), "tensor"),
    )
    out_specs = (
        P(("groups", "seq"), "tensor"),
        P(("groups", "seq"), "tensor"),
        P(("groups", "seq"), "tensor"),
    )
    return jax.shard_map(step, mesh=mesh, in_specs=in_specs, out_specs=out_specs, check_vma=False)
```

```python
import functools
import math

import jax
import jax.numpy as jnp
from jax import lax
from jax.experimental import pallas as pl
from jax.experimental.pallas import tpu as pltpu
from jax.sharding import PartitionSpec as P

HD = 128


def blank_state(query_rows, head_count):
    return (
        jnp.full((head_count, query_rows), -1e30, jnp.float32),
        jnp.zeros((head_count, query_rows), jnp.float32),
        jnp.zeros((head_count, query_rows, HD), jnp.float32),
    )


def absorb(carried, queries, keyset, values, head_count):
    running, row_sum, numerator = carried
    query_rows = queries.shape[0]
    key_rows = keyset.shape[0]
    factor = 1.0 / math.sqrt(HD)
    query_heads = queries.reshape(query_rows, head_count, HD)
    for offset in range(0, key_rows, 1024):
        width_keys = min(1024, key_rows - offset)
        key_block = keyset[offset : offset + width_keys].reshape(width_keys, head_count, HD)
        value_block = values[offset : offset + width_keys].reshape(width_keys, head_count, HD)
        scores = (
            jnp.einsum("qhd,khd->hqk", query_heads, key_block, preferred_element_type=jnp.float32)
            * factor
        )
        highest = jnp.maximum(running, jnp.max(scores, axis=2))
        raised = jnp.exp(scores - highest[:, :, None])
        shrink = jnp.exp(running - highest)
        row_sum = row_sum * shrink + jnp.sum(raised, axis=2)
        numerator = numerator * shrink[:, :, None] + jnp.einsum(
            "hqk,khd->hqd",
            raised.astype(jnp.bfloat16),
            value_block,
            preferred_element_type=jnp.float32,
        )
        running = highest
    return (running, row_sum, numerator)


def finish(carried, head_count):
    running, row_sum, numerator = carried
    result = numerator / row_sum[:, :, None]
    return result.transpose(1, 0, 2).reshape(result.shape[1], head_count * HD).astype(jnp.bfloat16)


def local(
    video_query,
    video_key,
    video_value,
    video_stream,
    out_weight,
    cross_query,
    audio_key,
    audio_value,
    audio_query,
    cross_key,
    cross_value,
):
    local_heads = video_query.shape[1] // HD
    query_rows = video_query.shape[0]
    pieces = (
        lax.all_gather(video_key, "seq", axis=0, tiled=True),
        lax.all_gather(video_value, "seq", axis=0, tiled=True),
    )
    carried_video = absorb(
        blank_state(query_rows, local_heads), video_query, pieces[0], pieces[1], local_heads
    )
    attended = finish(carried_video, local_heads)
    projected = jnp.dot(attended, out_weight, preferred_element_type=jnp.float32)
    summed = lax.psum_scatter(
        projected.astype(jnp.bfloat16), "tensor", scatter_dimension=1, tiled=True
    ).astype(jnp.float32)
    video_next = (video_stream.astype(jnp.float32) + summed).astype(jnp.bfloat16)
    cross_heads = cross_query.shape[1] // HD
    every_key, every_value = (
        lax.all_gather(audio_key, "seq", axis=0, tiled=True),
        lax.all_gather(audio_value, "seq", axis=0, tiled=True),
    )
    carried_audio = absorb(
        blank_state(cross_query.shape[0], cross_heads),
        cross_query,
        every_key,
        every_value,
        cross_heads,
    )
    video_cross = finish(carried_audio, cross_heads)
    pieces = (
        lax.all_gather(cross_key, "seq", axis=0, tiled=True),
        lax.all_gather(cross_value, "seq", axis=0, tiled=True),
    )
    carried_cross = absorb(
        blank_state(audio_query.shape[0], cross_heads),
        audio_query,
        pieces[0],
        pieces[1],
        cross_heads,
    )
    audio_cross = finish(carried_cross, cross_heads)
    return (video_next, video_cross, audio_cross)


MESH = pl.DeviceIdType.MESH
NT = (((1,), (1,)), ((), ()))
WIDE = 512
FIRST = 4


def softmax_parts(queries, keyset, values):
    scores = lax.dot_general(queries, keyset, NT, preferred_element_type=jnp.float32) * (
        1.0 / math.sqrt(HD)
    )
    highest = jnp.max(scores, axis=1, keepdims=True)
    raised = jnp.exp(scores - highest)
    row_sum = jnp.sum(raised, axis=1, keepdims=True)
    numerator = jnp.dot(raised.astype(jnp.bfloat16), values, preferred_element_type=jnp.float32)
    return highest, row_sum, numerator


def block_kernel(
    seq,
    tensor,
    vq,
    vk,
    vv,
    vs,
    weight,
    cq,
    ak,
    av,
    aq,
    ck,
    cv,
    next_ref,
    vcross_ref,
    across_ref,
    qkv,
    heads_out,
    gathered,
    audio,
    partial,
    stats,
    partial_in,
    stats_in,
    cq_v,
    ck_v,
    cv_v,
    stream_v,
    weight_v,
    kept,
    pair_out,
    pair_in,
    far_out,
    far_in,
    kv_send,
    kv_recv,
    q_send,
    q_recv,
    own_sem,
    out_send,
    out_recv,
    audio_send,
    audio_recv,
    audio_own,
    part_send,
    part_recv,
    stat_send,
    stat_recv,
    load_sem,
    weight_sem,
    pair_send,
    pair_recv,
    far_send,
    far_recv,
):
    rows = vq.shape[0]
    share = vq.shape[1] // HD // seq
    cross_heads = cq.shape[1] // HD
    audio_rows = aq.shape[0]
    chips = tensor // 2
    width = next_ref.shape[1]
    pieces = width // WIDE
    cuts = row_cuts(rows)
    me = lax.axis_index("seq")
    place = lax.axis_index("tensor")
    core = lax.rem(place, 2)
    chip = place // 2
    sibling = chip * 2 + (1 - core)
    peers = [lax.rem(me + d, seq) for d in range(1, seq)]
    far_chips = [lax.rem(chip + d, chips) for d in range(chips)]

    my_rows = pl.ds(pl.multiple_of(me * rows, rows), rows)
    my_audio = pl.ds(pl.multiple_of(me * audio_rows, audio_rows), audio_rows)

    def head_cols(owner, h):
        return pl.ds(pl.multiple_of((owner * share + h) * HD, HD), HD)

    local_copies = []
    for h in range(share):
        for kind, ref in enumerate((vk, vv, vq)):
            copy = pltpu.make_async_copy(
                ref.at[:, head_cols(me, h)], qkv.at[kind, h, my_rows], own_sem.at[kind, h]
            )
            copy.start()
            local_copies.append(copy)
    audio_copies = []
    for kind, ref in enumerate((ak, av, aq)):
        copy = pltpu.make_async_copy(ref, audio.at[kind, my_audio], audio_own.at[kind])
        copy.start()
        audio_copies.append(copy)
    loads = []
    for i, (ref, dst) in enumerate(((cq, cq_v), (ck, ck_v), (cv, cv_v), (vs, stream_v))):
        copy = pltpu.make_async_copy(ref, dst, load_sem.at[i])
        copy.start()
        loads.append(copy)

    barrier = pltpu.get_barrier_semaphore()
    for p in peers:
        pl.semaphore_signal(barrier, inc=1, device_id={"seq": p}, device_id_type=MESH)
    pl.semaphore_signal(barrier, inc=1, device_id={"tensor": sibling}, device_id_type=MESH)
    for d in range(1, chips):
        pl.semaphore_signal(
            barrier, inc=1, device_id={"tensor": far_chips[d] * 2 + core}, device_id_type=MESH
        )
    pl.semaphore_wait(barrier, seq - 1 + chips)

    sends = []

    def to_seq(src, dst, send_sem, recv_sem, p):
        return pltpu.make_async_remote_copy(
            src_ref=src,
            dst_ref=dst,
            send_sem=send_sem,
            recv_sem=recv_sem,
            device_id={"seq": p},
            device_id_type=MESH,
        )

    def launch(copy):
        copy.start()
        sends.append(copy)

    def cut_of(p, r):
        start, size = cuts[r]
        return pl.ds(pl.multiple_of(p * rows + start, 16), size)

    def send_queries(r):
        start, size = cuts[r]
        for h in range(share):
            for p in peers:
                launch(
                    to_seq(
                        vq.at[pl.ds(start, size), head_cols(p, h)],
                        qkv.at[2, h, cut_of(me, r)],
                        q_send.at[r, h, p],
                        q_recv.at[r, h, me],
                        p,
                    )
                )

    def rows_of(p):
        return pl.ds(pl.multiple_of(p * rows, rows), rows)

    def audio_rows_of(p):
        return pl.ds(pl.multiple_of(p * audio_rows, audio_rows), audio_rows)

    def audio_hop(step, way):
        shard = lax.rem(me - way * step + seq, seq)
        here = audio_rows_of(shard)
        return to_seq(
            audio.at[:, here],
            audio.at[:, here],
            audio_send.at[step, (way + 1) // 2],
            audio_recv.at[shard],
            lax.rem(me + way + seq, seq),
        )

    def on_line(step, way):
        source, target = me - way * step, me + way
        return (source >= 0) & (source < seq) & (target >= 0) & (target < seq)

    def pass_audio(step):
        for way in (1, -1):

            @pl.when(on_line(step, way))
            def _():
                copy = audio_hop(step, way)
                if step:
                    copy.wait_recv()
                copy.start()

    def end_audio():
        for step in range(1, seq):
            for way in (1, -1):
                source, target = me - way * step, me + way
                last = (target < 0) | (target >= seq)

                @pl.when((source >= 0) & (source < seq) & last)
                def _():
                    audio_hop(step, way).wait_recv()

    for copy in audio_copies:
        copy.wait()
    pass_audio(0)
    for h in range(share):
        for kind, ref in enumerate((vk, vv)):
            for p in peers:
                launch(
                    to_seq(
                        ref.at[:, head_cols(p, h)],
                        qkv.at[kind, h, my_rows],
                        kv_send.at[kind, h, p],
                        kv_recv.at[kind, h, me],
                        p,
                    )
                )
    pass_audio(1)
    send_queries(0)
    for r in range(1, len(cuts)):
        send_queries(r)

    weight_copy = pltpu.make_async_copy(weight, weight_v, weight_sem)
    weight_copy.start()

    def wait_from(src, dst, send_sem, recv_sem, p):
        to_seq(src, dst, send_sem, recv_sem, p).wait_recv()

    def wait_keys():
        for copy in local_copies:
            copy.wait()
        for h in range(share):
            for kind, ref in enumerate((vk, vv)):
                for p in peers:
                    wait_from(
                        ref.at[:, head_cols(p, h)],
                        qkv.at[kind, h, rows_of(p)],
                        kv_send.at[kind, h, p],
                        kv_recv.at[kind, h, p],
                        p,
                    )

    def attend_rows(r):
        start, size = cuts[r]
        here = pl.ds(start, size)
        for h in range(share):
            keyset, values = qkv[0, h], qkv[1, h]
            for p in peers + [me]:
                if p is not me:
                    wait_from(
                        vq.at[here, head_cols(p, h)],
                        qkv.at[2, h, cut_of(p, r)],
                        q_send.at[r, h, p],
                        q_recv.at[r, h, p],
                        p,
                    )
                _, row_sum, numerator = softmax_parts(qkv[2, h, cut_of(p, r)], keyset, values)
                result = (numerator / row_sum).astype(jnp.bfloat16)
                if p is me:
                    gathered[h, me, here] = result
                else:
                    heads_out[h, p, here] = result
                    launch(
                        to_seq(
                            heads_out.at[h, p, here],
                            gathered.at[h, me, here],
                            out_send.at[r, h, p],
                            out_recv.at[r, h, me],
                            p,
                        )
                    )

    def cross_parts():
        for i in range(3):
            loads[i].wait()
        end_audio()
        lane = lax.broadcasted_iota(jnp.int32, (seq * audio_rows, HD), 1)
        held = jnp.zeros((seq * audio_rows, HD), jnp.float32)
        for c in range(cross_heads):
            cols = slice(c * HD, (c + 1) * HD)
            highest, row_sum, numerator = softmax_parts(audio[2, :, cols], ck_v[:, cols], cv_v[:, cols])
            held = jnp.where(lane == c, highest, held)
            held = jnp.where(lane == cross_heads + c, row_sum, held)
            partial[:, cols] = numerator.astype(jnp.bfloat16)
        stats[...] = held
        for p in peers:
            for src, dst, s_sem, r_sem in (
                (partial, partial_in, part_send, part_recv),
                (stats, stats_in, stat_send, stat_recv),
            ):
                copy = pltpu.make_async_remote_copy(
                    src_ref=src.at[audio_rows_of(p)],
                    dst_ref=dst.at[me],
                    send_sem=s_sem.at[p],
                    recv_sem=r_sem.at[me],
                    device_id={"seq": p},
                    device_id_type=MESH,
                )
                copy.start()
                sends.append(copy)
        for c in range(cross_heads):
            cols = slice(c * HD, (c + 1) * HD)
            _, row_sum, numerator = softmax_parts(cq_v[:, cols], audio[0, :, cols], audio[1, :, cols])
            vcross_ref[:, cols] = (numerator / row_sum).astype(jnp.bfloat16)

    def cross_finish():
        for p in peers:
            wait_from(partial.at[audio_rows_of(p)], partial_in.at[p], part_send.at[p], part_recv.at[p], p)
            wait_from(stats.at[audio_rows_of(p)], stats_in.at[p], stat_send.at[p], stat_recv.at[p], p)
        held = [stats[my_audio, :]] + [stats_in[p] for p in peers]
        for c in range(cross_heads):
            cols = slice(c * HD, (c + 1) * HD)
            parts = [partial[my_audio, cols]] + [partial_in[p, :, cols] for p in peers]
            tops = [s[:, c : c + 1] for s in held]
            sums = [s[:, cross_heads + c : cross_heads + c + 1] for s in held]
            highest = functools.reduce(jnp.maximum, tops)
            factors = [jnp.exp(t - highest) for t in tops]
            row_sum = sum(f * s for f, s in zip(factors, sums))
            numerator = sum(f * n.astype(jnp.float32) for f, n in zip(factors, parts))
            across_ref[:, cols] = (numerator / row_sum).astype(jnp.bfloat16)

    def wait_heads(r):
        here = pl.ds(*cuts[r])
        for h in range(share):
            for p in peers:
                wait_from(
                    heads_out.at[h, p, here],
                    gathered.at[h, p, here],
                    out_send.at[r, h, p],
                    out_recv.at[r, h, p],
                    p,
                )
        return jnp.concatenate(
            [gathered[h, p, here] for p in range(seq) for h in range(share)], axis=1
        )

    def product(attended, d, side, j):
        target = far_chips[d] * 2 + (core if side else 1 - core)
        cols = pl.ds(pl.multiple_of(target * width + j * WIDE, WIDE), WIDE)
        return jnp.dot(attended, weight_v[:, cols], preferred_element_type=jnp.float32)

    def pair_copy(r, d, j):
        here = pl.ds(*cuts[r])
        return pltpu.make_async_remote_copy(
            src_ref=pair_out.at[d, j, here],
            dst_ref=pair_in.at[d, j, here],
            send_sem=pair_send.at[r, d, j],
            recv_sem=pair_recv.at[r, d, j],
            device_id={"tensor": sibling},
            device_id_type=MESH,
        )

    def far_copy(r, d, j):
        here = pl.ds(*cuts[r])
        return pltpu.make_async_remote_copy(
            src_ref=far_out.at[d - 1, j, here],
            dst_ref=far_in.at[d - 1, j, here],
            send_sem=far_send.at[r, d - 1, j],
            recv_sem=far_recv.at[r, d - 1, j],
            device_id={"tensor": far_chips[d] * 2 + core},
            device_id_type=MESH,
        )

    def share_rows(r):
        here = pl.ds(*cuts[r])
        attended = wait_heads(r)
        if r == 0:
            weight_copy.wait()
        steps = [(d, j) for d in range(1, chips) for j in range(pieces)]
        for d, j in steps:
            pair_out[d, j, here] = product(attended, d, 0, j).astype(jnp.bfloat16)
            launch(pair_copy(r, d, j))
        for d, j in steps:
            mine = product(attended, d, 1, j)
            pair_copy(r, d, j).wait_recv()
            far_out[d - 1, j, here] = (mine + pair_in[d, j, here].astype(jnp.float32)).astype(
                jnp.bfloat16
            )
            launch(far_copy(r, d, j))
        for j in range(pieces):
            pair_out[0, j, here] = product(attended, 0, 0, j).astype(jnp.bfloat16)
            launch(pair_copy(r, 0, j))
        for j in range(pieces):
            block = slice(j * WIDE, (j + 1) * WIDE)
            kept[here, block] = product(attended, 0, 1, j) + stream_v[here, block].astype(jnp.float32)

    def close_rows(r):
        here = pl.ds(*cuts[r])
        for j in range(pieces):
            block = slice(j * WIDE, (j + 1) * WIDE)
            pair_copy(r, 0, j).wait_recv()
            value = kept[here, block] + pair_in[0, j, here].astype(jnp.float32)
            for d in range(1, chips):
                far_copy(r, d, j).wait_recv()
                value = value + far_in[d - 1, j, here].astype(jnp.float32)
            next_ref[here, block] = value.astype(jnp.bfloat16)

    wait_keys()
    for step in range(2, seq - 1):
        pass_audio(step)
    for r in range(len(cuts)):
        attend_rows(r)
    cross_parts()
    loads[3].wait()
    for r in range(len(cuts)):
        share_rows(r)
    cross_finish()
    for r in range(len(cuts)):
        close_rows(r)
    for copy in sends:
        copy.wait_send()
    for step in range(seq - 1):
        for way in (1, -1):

            @pl.when(on_line(step, way))
            def _():
                audio_hop(step, way).wait_send()


def row_cuts(rows):
    first = max(rows * FIRST // 4 // 16 * 16, 16)
    return [(0, first), (first, rows - first)] if first < rows else [(0, rows)]


def write_out(*refs):
    half = len(refs) // 2
    for src, dst in zip(refs[:half], refs[half:]):
        dst[...] = src[...]


def fused(seq, tensor, *operands):
    vq, vk, vv, vs, weight, cq, ak, av, aq, ck, cv = operands
    rows, features = vq.shape
    share = features // HD // seq
    audio_rows, cross_width = aq.shape
    chips = tensor // 2
    width = weight.shape[1] // tensor
    pieces = width // WIDE
    groups = len(row_cuts(rows))
    bf16, f32, dma = jnp.bfloat16, jnp.float32, pltpu.SemaphoreType.DMA
    shapes = tuple(jax.ShapeDtypeStruct(x.shape, bf16) for x in (vs, cq, aq))
    whole = pl.BlockSpec(memory_space=pltpu.VMEM)
    results = pl.pallas_call(
        functools.partial(block_kernel, seq, tensor),
        out_shape=tuple(pltpu.VMEM(x.shape, bf16) for x in (vs, cq, aq)),
        in_specs=[pl.BlockSpec(memory_space=pltpu.HBM)] * 11,
        out_specs=(whole,) * 3,
        scratch_shapes=[
            pltpu.VMEM((3, share, seq * rows, HD), bf16),
            pltpu.VMEM((share, seq, rows, HD), bf16),
            pltpu.VMEM((share, seq, rows, HD), bf16),
            pltpu.VMEM((3, seq * audio_rows, cross_width), bf16),
            pltpu.VMEM((seq * audio_rows, cross_width), bf16),
            pltpu.VMEM((seq * audio_rows, HD), f32),
            pltpu.VMEM((seq, audio_rows, cross_width), bf16),
            pltpu.VMEM((seq, audio_rows, HD), f32),
            pltpu.VMEM(cq.shape, bf16),
            pltpu.VMEM(ck.shape, bf16),
            pltpu.VMEM(cv.shape, bf16),
            pltpu.VMEM(vs.shape, bf16),
            pltpu.VMEM(weight.shape, bf16),
            pltpu.VMEM(vs.shape, f32),
            pltpu.VMEM((chips, pieces, rows, WIDE), bf16),
            pltpu.VMEM((chips, pieces, rows, WIDE), bf16),
            pltpu.VMEM((max(chips - 1, 1), pieces, rows, WIDE), bf16),
            pltpu.VMEM((max(chips - 1, 1), pieces, rows, WIDE), bf16),
            dma((2, share, seq)),
            dma((2, share, seq)),
            dma((groups, share, seq)),
            dma((groups, share, seq)),
            dma((3, share)),
            dma((groups, share, seq)),
            dma((groups, share, seq)),
            dma((seq, 2)),
            dma((seq,)),
            dma((3,)),
            dma((seq,)),
            dma((seq,)),
            dma((seq,)),
            dma((seq,)),
            dma((4,)),
            dma(()),
            dma((groups, chips, pieces)),
            dma((groups, chips, pieces)),
            dma((groups, max(chips - 1, 1), pieces)),
            dma((groups, max(chips - 1, 1), pieces)),
        ],
        compiler_params=pltpu.CompilerParams(
            collective_id=0, has_side_effects=True, vmem_limit_bytes=60000000
        ),
    )(*operands)
    return pl.pallas_call(
        write_out,
        out_shape=shapes,
        in_specs=[whole] * 3,
        out_specs=(whole,) * 3,
        compiler_params=pltpu.CompilerParams(vmem_limit_bytes=8 * 2**20),
    )(*results)


def fits(mesh, operands):
    seq, tensor = mesh.shape["seq"], mesh.shape["tensor"]
    vq, weight, cq, aq = operands[0], operands[4], operands[5], operands[8]
    return (
        seq > 1
        and (vq.shape[1] // HD) % seq == 0
        and tensor % 2 == 0
        and (weight.shape[1] // tensor) % WIDE == 0
        and aq.shape[0] % 16 == 0
        and vq.shape[0] % 16 == 0
        and 2 * (cq.shape[1] // HD) <= HD
        and weight.size * 2 <= 10 * 2**20
        and vq.shape[0] <= 128
        and seq <= 8
    )


def solution(mesh):
    def step(*operands):
        if fits(mesh, operands):
            return fused(mesh.shape["seq"], mesh.shape["tensor"], *operands)
        return local(*operands)

    in_specs = (
        P(("groups", "seq"), "tensor"),
        P(("groups", "seq"), "tensor"),
        P(("groups", "seq"), "tensor"),
        P(("groups", "seq"), "tensor"),
        P("tensor", None),
        P(("groups", "seq"), "tensor"),
        P(("groups", "seq"), "tensor"),
        P(("groups", "seq"), "tensor"),
        P(("groups", "seq"), "tensor"),
        P(("groups", "seq"), "tensor"),
        P(("groups", "seq"), "tensor"),
    )
    out_specs = (
        P(("groups", "seq"), "tensor"),
        P(("groups", "seq"), "tensor"),
        P(("groups", "seq"), "tensor"),
    )
    return jax.shard_map(step, mesh=mesh, in_specs=in_specs, out_specs=out_specs, check_vma=False)
```
